256 devices in a mesh: row: 16 (over x_lo, z), col: 16 (over x_hi, y, core).
Axes of the slice: x: 4 (x_hi: 2, x_lo: 2; x = x_hi * 2 + x_lo), y: 4, z: 8, core: 2. Of those that a mesh axis runs over, the one named last changes fastest.
Arguments:
- cov: float32 [16384, 16384], P('row', 'col'), as said below
- noise: float32 [16384, 16384], P('row', 'col'), as said below
- diffusivity: float32 [128, 128], P('row'), may hold values from 0.25 to 1
- wind_x: float32 [128, 128], P('row'), may hold values from -1 to 1
- wind_y: float32 [128, 128], P('row'), may hold values from -1 to 1
Outputs:
- cov_next: float32 [16384, 16384], P('row', 'col')
The draws below stay inside these ranges and needn't reach their ends.
Inputs may be any that keep to these rules, and one draw needn't show every extreme that they name: cov is symmetric. noise is symmetric.
All inputs are finite; a program needn't handle non-finite values.
Results may differ from the reference program's by a relative error of at most 0.00002.
Values sent between devices are 32-bit elements; how exact they have to be, the bound alone decides.
No kernel may reach another device: no remote copies, remote signals or barrier semaphores. Data moves between devices by JAX's collectives and lax.ppermute only.
A program may use at most 192 MiB of HBM per device.

```python
import math
import jax
import jax.numpy as jnp

G = 128
STATES = 16384


def draw_cov(key, part):
    base = jax.random.normal(key, (STATES, STATES), jnp.float32)
    return 0.5 * (base + base.T) + 3.0 * jnp.eye(STATES, dtype=jnp.float32)


def draw_noise(key, part):
    base = 2.0 * jax.random.normal(key, (STATES, STATES), jnp.float32)
    return 0.5 * (base + base.T) + jnp.eye(STATES, dtype=jnp.float32)


def levels(rng, shape, cuts, least, largest):
    def one(dim, shards_of):
        steps = jax.random.uniform(jax.random.fold_in(jax.random.fold_in(rng, 6), dim), (shards_of,), jnp.float32, least / len(cuts), largest / len(cuts))
        return jnp.repeat(jnp.exp(steps), shape[dim] // shards_of).reshape((-1,) + (1,) * (len(shape) - dim - 1))

    loudness = one(*cuts[0])
    for cut in cuts[1:]:
        loudness = loudness * one(*cut)
    return loudness


def setup_inputs(seed: int = 0) -> dict:
    key_of = jax.random.split(jax.random.key(seed), 6)
    cov = draw_cov(jax.random.fold_in(key_of[5], 71), 0)
    noise = draw_noise(jax.random.fold_in(key_of[5], 71), 0)
    diffusivity = jnp.clip(jnp.exp(math.log(1.0) - 1.3862944 * jax.random.uniform(key_of[2], (G, G), jnp.float32) ** levels(key_of[2], (G, G), ((0, 16),), -0.2, 0.2)), 0.25, 1.0)
    wind_x = jnp.clip(jax.random.uniform(key_of[3], (G, G), jnp.float32, -1.0, 1.0) * levels(key_of[3], (G, G), ((0, 16),), -0.4, 0.0), -1.0, 1.0)
    wind_y = jnp.clip(jax.random.uniform(key_of[4], (G, G), jnp.float32, -1.0, 1.0) * levels(key_of[4], (G, G), ((0, 16),), -0.4, 0.0), -1.0, 1.0)
    return {"cov": cov, "noise": noise, "diffusivity": diffusivity, "wind_x": wind_x, "wind_y": wind_y}


OFFSETS = ((0, 0), (1, 0), (-1, 0), (0, 1), (0, -1), (1, 1), (1, -1), (-1, 1), (-1, -1))
time_step = 0.1


def stencil_weights(kappa, flow_x, flow_y):
    edge = (4.0 / 6.0) * kappa
    corner = kappa / 6.0
    return jnp.stack([(-20.0 / 6.0) * kappa, edge - 0.5 * flow_x, edge + 0.5 * flow_x,
                      edge - 0.5 * flow_y, edge + 0.5 * flow_y, corner, corner, corner, corner])


def row_term(padded, weights):
    count = weights.shape[1]
    side = weights.shape[2]
    wide = jnp.pad(padded, ((0, 0), (1, 1), (0, 0)))
    total = jnp.zeros((count, side, padded.shape[2]), jnp.float32)
    for index, (step_x, step_y) in enumerate(OFFSETS):
        piece = wide[1 + step_x:1 + step_x + count, 1 + step_y:1 + step_y + side, :]
        total = total + weights[index][:, :, None] * piece
    return total


def col_term(padded, weights):
    count = weights.shape[1]
    side = weights.shape[2]
    wide = jnp.pad(padded, ((0, 0), (0, 0), (1, 1)))
    total = jnp.zeros((padded.shape[0], count, side), jnp.float32)
    for index, (step_x, step_y) in enumerate(OFFSETS):
        piece = wide[:, 1 + step_x:1 + step_x + count, 1 + step_y:1 + step_y + side]
        total = total + weights[index][None, :, :] * piece
    return total


def derive(field, noise, weights):
    states = field.shape[0]
    along_rows = row_term(jnp.pad(field.reshape(G, G, states), ((1, 1), (0, 0), (0, 0))), weights)
    along_cols = col_term(jnp.pad(field.reshape(states, G, G), ((0, 0), (1, 1), (0, 0))), weights)
    return along_rows.reshape(states, states) + along_cols.reshape(states, states) + noise


def reference(cov, noise, diffusivity, wind_x, wind_y):
    weights = stencil_weights(diffusivity, wind_x, wind_y)
    first = derive(cov, noise, weights)
    middle = cov + time_step * first
    second = derive(middle, noise, weights)
    return cov + (0.5 * time_step) * (first + second)
```

```python
import functools

import jax
import jax.numpy as jnp
from jax import lax
from jax.experimental import pallas as pl
from jax.experimental.pallas import tpu as pltpu
from jax.sharding import PartitionSpec as P

T = 128
LANES = 128
F32 = jnp.float32
STEP = 0.1
SECOND = 0.5 * STEP * STEP


def seven(kappa, flow_x, flow_y):
    edge = (4.0 / 6.0) * kappa
    corner = kappa / 6.0
    at = lax.broadcasted_iota(jnp.int32, kappa.shape, 1)

    def from_above(v):
        return jnp.where(at == 0, 0.0, pltpu.roll(v, 1, 1))

    def from_below(v):
        return jnp.where(at == T - 1, 0.0, pltpu.roll(v, T - 1, 1))

    return [
        (-20.0 / 6.0) * kappa,
        edge - 0.5 * flow_x,
        edge + 0.5 * flow_x,
        from_above(edge - 0.5 * flow_y),
        from_above(corner),
        from_below(edge + 0.5 * flow_y),
        from_below(corner),
    ]


def columns(lists):
    rows = list(lists)
    have = 8 * len(rows)
    if have < LANES:
        rows.append(jnp.zeros((LANES - have, LANES), F32))
    return jnp.concatenate(rows, axis=0).T


def spread(cols, j, x):
    return jnp.broadcast_to(cols[:, 8 * j + x : 8 * j + x + 1], (T, LANES))


def shifted(up, down, axis):
    return pltpu.roll(up, T - 1, axis) + pltpu.roll(down, 1, axis)


def full(mid, low, high, w, axis):
    both = low + high
    return w[0] * mid + w[1] * high + w[2] * low + shifted(w[3] * mid + w[4] * both, w[5] * mid + w[6] * both, axis)


def off(value, w, side, axis):
    return w[side] * value + shifted(w[4] * value, w[6] * value, axis)


def own(value, w, axis):
    return w[0] * value + shifted(w[3] * value, w[5] * value, axis)


def tile(i):
    return slice(i * T, (i + 1) * T)


def at_tile(i):
    return pl.ds(pl.multiple_of(i * T, T), T)


def cp(**kw):
    return pltpu.CompilerParams(vmem_limit_bytes=48 << 20, **kw)


def vmem():
    return pl.BlockSpec(memory_space=pltpu.VMEM)


def hbm():
    return pl.BlockSpec(memory_space=pl.ANY)


def row_edges_body(pt, pb, qt, qb, k, u, w, top, bottom, wide):
    x_last = 7

    @pl.when(pl.program_id(0) == 0)
    def _():
        cols = columns(seven(k[...], u[...], w[...]))
        for j in range(7):
            wide[0, j] = spread(cols, j, 0)
            wide[1, j] = spread(cols, j, x_last)

    for h in range(pt.shape[1] // T):
        lanes = tile(h)
        for m, n, q, out, i, side in (
            (pt[0:T, lanes], pt[T : 2 * T, lanes], qt[:, lanes], top, 0, 1),
            (pb[T : 2 * T, lanes], pb[0:T, lanes], qb[:, lanes], bottom, 1, 2),
        ):
            e = [wide[i, j] for j in range(7)]
            out[0:T, lanes] = q + own(m, e, 0) + off(n, e, side, 0)
            out[T : T + 8, lanes] = jnp.zeros((8, T), F32)

    @pl.when(pl.program_id(0) == 0)
    def _():
        for out, x in ((top, 0), (bottom, x_last)):
            out[T : T + 1, 0:T] = k[x : x + 1, :]
            out[T : T + 1, T : 2 * T] = u[x : x + 1, :]


def row_edges(cov, noise, k, u, w):
    n = cov.shape[1]
    step = 256
    last = cov.shape[0] // T
    small = pl.BlockSpec((8, T), lambda i: (0, 0))
    out = jax.ShapeDtypeStruct((T + 8, n), F32)
    return pl.pallas_call(
        row_edges_body,
        grid=(n // step,),
        in_specs=[
            pl.BlockSpec((2 * T, step), lambda i: (0, i)),
            pl.BlockSpec((2 * T, step), lambda i: (last // 2 - 1, i)),
            pl.BlockSpec((T, step), lambda i: (0, i)),
            pl.BlockSpec((T, step), lambda i: (last - 1, i)),
            small,
            small,
            small,
        ],
        out_specs=[pl.BlockSpec((T + 8, step), lambda i: (0, i))] * 2,
        out_shape=[out, out],
        scratch_shapes=[pltpu.VMEM((2, 7, T, T), F32)],
        compiler_params=cp(),
        name="row_edges",
    )(cov, cov, noise, noise, k, u, w)


def col_edges_body(pleft, pright, qleft, qright, upl, upr, dnl, dnr, k, u, w, cw, left, right):
    cols = columns(seven(k[...], u[...], w[...]))
    ck, cu, cv = cw[0:8, :], cw[8:16, :], cw[16:24, :]
    v = seven(ck, cu, cv)
    zero = jnp.zeros((T, T), F32)
    for x in range(8):
        e = [spread(cols, j, x) for j in range(7)]
        for p, q, up, dn, out, h, near, far, side in (
            (pleft, qleft, upl, dnl, left, 0, tile(0), tile(1), 1),
            (pright, qright, upr, dnr, right, 7, tile(1), tile(0), 2),
        ):
            vh = [a[h : h + 1, :] for a in v]
            mid = p[tile(x), near]
            low = 2.0 * up[...] if x == 0 else p[tile(x - 1), near]
            high = 2.0 * dn[...] if x == 7 else p[tile(x + 1), near]
            value = q[tile(x), :] + full(mid, low, high, e, 0)
            value = value + own(mid, vh, 1) + off(p[tile(x), far], vh, side, 1)
            out[tile(x), 0:T] = mid
            out[tile(x), T : 2 * T] = value
    for out, h in ((left, 0), (right, 7)):
        out[8 * T : 8 * T + 8, :] = jnp.zeros((8, 2 * T), F32)
        out[8 * T : 8 * T + 1, 0:T] = ck[h : h + 1, :]
        out[8 * T : 8 * T + 1, T : 2 * T] = cu[h : h + 1, :]


def col_edges(cov, noise, up_p, dn_p, k, u, w, cw):
    rows, n = cov.shape
    last = n // T - 1
    one = lambda i, j: pl.BlockSpec((T, T), lambda s: (i, j))
    small = pl.BlockSpec((8, T), lambda s: (0, 0))
    out = jax.ShapeDtypeStruct((rows + 8, 2 * T), F32)
    return pl.pallas_call(
        col_edges_body,
        grid=(1,),
        in_specs=[
            pl.BlockSpec((rows, 2 * T), lambda s: (0, 0)),
            pl.BlockSpec((rows, 2 * T), lambda s: (0, n // (2 * T) - 1)),
            pl.BlockSpec((rows, T), lambda s: (0, 0)),
            pl.BlockSpec((rows, T), lambda s: (0, last)),
            one(0, 0),
            one(0, last),
            one(0, 0),
            one(0, last),
            small,
            small,
            small,
            pl.BlockSpec((24, T), lambda s: (0, 0)),
        ],
        out_specs=[pl.BlockSpec((rows + 8, 2 * T), lambda s: (0, 0))] * 2,
        out_shape=[out, out],
        compiler_params=cp(),
        name="col_edges",
    )(cov, cov, noise, noise, up_p, up_p, dn_p, dn_p, k, u, w, cw)


def block_body(p_hbm, q_hbm, up, dn, k, u, w, cw, out_hbm, pe, fe, qo, wide, v_s, sem_p, sem_q, sem_o):
    n = 8 * T

    def load_p(x):
        return pltpu.make_async_copy(p_hbm.at[tile(x), :], pe.at[pl.ds((x + 1) * T, T), pl.ds(T, n)], sem_p.at[x])

    def load_q(x):
        return pltpu.make_async_copy(q_hbm.at[tile(x), :], qo.at[tile(x), :], sem_q.at[x])

    def save(x):
        return pltpu.make_async_copy(qo.at[tile(x), :], out_hbm.at[tile(x), :], sem_o.at[x])

    halo_u = pltpu.make_async_copy(up, pe.at[pl.ds(0, T), pl.ds(T, n)], sem_p.at[8])
    halo_d = pltpu.make_async_copy(dn, pe.at[pl.ds(9 * T, T), pl.ds(T, n)], sem_p.at[9])
    halo_u.start()
    for x in range(8):
        load_p(x).start()
        load_q(x).start()
    halo_d.start()
    pe[:, 0:T] = jnp.zeros((10 * T, T), F32)
    pe[:, 9 * T : 10 * T] = jnp.zeros((10 * T, T), F32)
    fe[:, 0:T] = jnp.zeros((10 * T, T), F32)
    fe[:, 9 * T : 10 * T] = jnp.zeros((10 * T, T), F32)
    fe[0:T, T : 9 * T] = jnp.zeros((T, n), F32)
    fe[9 * T : 10 * T, T : 9 * T] = jnp.zeros((T, n), F32)
    cols = columns(seven(k[...], u[...], w[...]))
    v = seven(cw[0:8, :], cw[8:16, :], cw[16:24, :])
    for x in range(8):
        for j in range(7):
            wide[x, j] = spread(cols, j, x)
            v_s[x, j] = jnp.broadcast_to(v[j][x : x + 1, :], (8, T))

    def apply(src, x, h):
        e = [wide[x, j] for j in range(7)]
        vh = [v_s[h, j, 0:1, :] for j in range(7)]
        row = lambda i: pl.ds(pl.multiple_of(i * T, T), T)
        mid = src[row(x + 1), row(h + 1)]
        a = full(mid, src[row(x), row(h + 1)], src[row(x + 2), row(h + 1)], e, 0)
        b = full(mid, src[row(x + 1), row(h)], src[row(x + 1), row(h + 2)], vh, 1)
        return mid, a + b

    def first(x):
        @pl.loop(0, 8)
        def _(h):
            _, value = apply(pe, x, h)
            fe[pl.ds((x + 1) * T, T), at_tile(h + 1)] = value + qo[tile(x), at_tile(h)]

    def second(x):
        @pl.loop(0, 8)
        def _(h):
            mid, value = apply(fe, x, h)
            qo[tile(x), at_tile(h)] = pe[pl.ds((x + 1) * T, T), at_tile(h + 1)] + STEP * mid + SECOND * value

    halo_u.wait()
    load_p(0).wait()
    for x in range(9):
        if x < 8:
            if x < 7:
                load_p(x + 1).wait()
            else:
                halo_d.wait()
            load_q(x).wait()
            first(x)
        if x > 0:
            second(x - 1)
            save(x - 1).start()
    for x in range(8):
        save(x).wait()


def block(cov, noise, up_p, dn_p, k, u, w, cw):
    return pl.pallas_call(
        block_body,
        in_specs=[hbm(), hbm(), hbm(), hbm(), vmem(), vmem(), vmem(), vmem()],
        out_specs=hbm(),
        out_shape=jax.ShapeDtypeStruct(cov.shape, F32),
        scratch_shapes=[
            pltpu.VMEM((10 * T, 10 * T), F32),
            pltpu.VMEM((10 * T, 10 * T), F32),
            pltpu.VMEM((8 * T, 8 * T), F32),
            pltpu.VMEM((8, 7, T, T), F32),
            pltpu.VMEM((8, 7, 8, T), F32),
            pltpu.SemaphoreType.DMA((10,)),
            pltpu.SemaphoreType.DMA((8,)),
            pltpu.SemaphoreType.DMA((8,)),
        ],
        compiler_params=cp(),
        name="block",
    )(cov, noise, up_p, dn_p, k, u, w, cw)


def row_halo_body(o_in, p, up, dn, gu, gd, k, u, w, cw, o_out, wide):
    s = pl.program_id(0)
    cols = columns(seven(k[...], u[...], w[...]))
    v = seven(cw[0:8, :], cw[8:16, :], cw[16:24, :])

    def side(x, xp, g, toward, back):
        beside = seven(
            jnp.broadcast_to(g[T : T + 1, 0:T], (8, T)), jnp.broadcast_to(g[T : T + 1, T : 2 * T], (8, T)), jnp.zeros((8, T), F32)
        )
        theirs = columns(beside)
        for j in (toward, 4, 6):
            wide[0, j] = spread(cols, j, x)
        for j in (back, 4, 6):
            wide[1, j] = spread(theirs, j, 0)
        e = [wide[0, j] for j in range(7)]
        f = [wide[1, j] for j in range(7)]
        zero = jnp.zeros((T, T), F32)
        for h in range(8):
            vh = [a[h : h + 1, :] for a in v]
            low = xp[:, tile(h - 1)] if h > 0 else zero
            high = xp[:, tile(h + 1)] if h < 7 else zero
            value = g[0:T, tile(h)] + off(p[:, tile(h)], f, back, 0) + full(xp[:, tile(h)], low, high, vh, 1)
            o_out[:, tile(h)] = o_in[:, tile(h)] + SECOND * off(value, e, toward, 0)

    @pl.when(s == 0)
    def _():
        side(0, up, gu, 2, 1)

    @pl.when(s == 1)
    def _():
        side(7, dn, gd, 1, 2)


def row_halo(out, cov, up_p, dn_p, gu, gd, k, u, w, cw):
    n = cov.shape[1]
    whole = lambda r, c: pl.BlockSpec((r, c), lambda s: (0, 0))
    edge = pl.BlockSpec((T, n), lambda s: (7 * s, 0))
    return pl.pallas_call(
        row_halo_body,
        grid=(2,),
        in_specs=[edge, edge, whole(T, n), whole(T, n), whole(T + 8, n), whole(T + 8, n), whole(8, T), whole(8, T), whole(8, T), whole(24, T)],
        out_specs=edge,
        out_shape=jax.ShapeDtypeStruct(out.shape, F32),
        scratch_shapes=[pltpu.VMEM((2, 7, T, T), F32)],
        input_output_aliases={0: 0},
        compiler_params=cp(),
        name="row_halo",
    )(out, cov, up_p, dn_p, gu, gd, k, u, w, cw)


def col_halo_body(o_in, p, yl, yr, k, u, w, cw, o_out, d):
    s = pl.program_id(0)
    cols = columns(seven(k[...], u[...], w[...]))
    v = seven(cw[0:8, :], cw[8:16, :], cw[16:24, :])
    zero = jnp.zeros((T, T), F32)

    def side(y, h, h2, near, far, mine, toward, back):
        tail = pl.ds(8 * T, 1)
        beside = seven(
            jnp.broadcast_to(y[tail, 0:T], (8, T)), jnp.broadcast_to(y[tail, T : 2 * T], (8, T)), jnp.zeros((8, T), F32)
        )
        f = [a[0:1, :] for a in beside]
        vh = [a[h : h + 1, :] for a in v]
        v2 = [a[h2 : h2 + 1, :] for a in v]
        for x in range(8):
            d[tile(x), :] = off(y[tile(x), 0:T], vh, toward, 1)
        for x in range(8):
            e = [spread(cols, j, x) for j in range(7)]
            mid = d[tile(x), :]
            low = d[tile(x - 1), :] if x > 0 else zero
            high = d[tile(x + 1), :] if x < 7 else zero
            beyond = y[tile(x), T : 2 * T] + off(p[tile(x), mine], f, back, 1)
            value = own(mid, vh, 1) + full(mid, low, high, e, 0) + off(beyond, vh, toward, 1)
            o_out[tile(x), near] = o_in[tile(x), near] + STEP * mid + SECOND * value
            o_out[tile(x), far] = o_in[tile(x), far] + SECOND * off(mid, v2, toward, 1)

    @pl.when(s == 0)
    def _():
        side(yl, 0, 1, tile(0), tile(1), tile(0), 2, 1)

    @pl.when(s == 1)
    def _():
        side(yr, 7, 6, tile(1), tile(0), tile(0), 1, 2)


def col_halo(out, cov, yl, yr, k, u, w, cw):
    rows, n = cov.shape
    whole = lambda r, c: pl.BlockSpec((r, c), lambda s: (0, 0))
    edge = pl.BlockSpec((rows, 2 * T), lambda s: (0, (n // (2 * T) - 1) * s))
    return pl.pallas_call(
        col_halo_body,
        grid=(2,),
        in_specs=[
            edge,
            pl.BlockSpec((rows, T), lambda s: (0, (n // T - 1) * s)),
            whole(rows + 8, 2 * T),
            whole(rows + 8, 2 * T),
            whole(8, T),
            whole(8, T),
            whole(8, T),
            whole(24, T),
        ],
        out_specs=edge,
        out_shape=jax.ShapeDtypeStruct(out.shape, F32),
        scratch_shapes=[pltpu.VMEM((rows, T), F32)],
        input_output_aliases={0: 0},
        compiler_params=cp(),
        name="col_halo",
    )(out, cov, yl, yr, k, u, w, cw)


@functools.cache
def weight_route(n):
    def place(r, c):
        half = n // 2
        return (2 * (c // half) + r // half, (c % half) // 2, r % half, c % 2)

    def far(a, b):
        ring = lambda d, size: min(d % size, -d % size)
        return ring(a[0] - b[0], 4) + ring(a[1] - b[1], max(n // 4, 1)) + ring(a[2] - b[2], n // 2) + 0.5 * (a[3] != b[3])

    pairs = []
    for c in range(n):
        cost = [[far(place(r, c), place(c, f)) for f in range(n)] for r in range(n)]
        for limit in sorted({x for row in cost for x in row}):
            taken = {}

            def find(r, seen):
                for f in sorted(range(n), key=lambda f: cost[r][f]):
                    if cost[r][f] <= limit and f not in seen:
                        seen.add(f)
                        if f not in taken or find(taken[f], seen):
                            taken[f] = r
                            return True
                return False

            if all(find(r, set()) for r in range(n)):
                break
        pairs += [(c * n + f, r * n + c) for f, r in taken.items()]
    return sorted(pairs)


def per_device(cov, noise, k, u, w):
    rows = lax.axis_size("row")
    cols = lax.axis_size("col")
    n0, n1 = cov.shape
    up = lambda n: [(i, i + 1) for i in range(n - 1)]
    down = lambda n: [(i + 1, i) for i in range(n - 1)]
    from_up = lambda a: lax.ppermute(a, "row", up(rows))
    from_dn = lambda a: lax.ppermute(a, "row", down(rows))

    up_p = from_up(cov[n0 - T :, :])
    dn_p = from_dn(cov[:T, :])
    cw = lax.ppermute(jnp.concatenate([k, u, w], axis=0), ("row", "col"), weight_route(rows))
    top, bottom = row_edges(cov, noise, k, u, w)
    gu = from_up(bottom)
    gd = from_dn(top)
    up_p, dn_p, _, _ = lax.optimization_barrier((up_p, dn_p, top, bottom))
    left, right = col_edges(cov, noise, up_p, dn_p, k, u, w, cw)
    yl = lax.ppermute(right, "col", up(cols))
    yr = lax.ppermute(left, "col", down(cols))
    out = block(cov, noise, up_p, dn_p, k, u, w, cw)
    out = row_halo(out, cov, up_p, dn_p, gu, gd, k, u, w, cw)
    return col_halo(out, cov, yl, yr, k, u, w, cw)


def solution(mesh):
    return jax.shard_map(
        per_device,
        mesh=mesh,
        in_specs=(P("row", "col"), P("row", "col"), P("row", None), P("row", None), P("row", None)),
        out_specs=P("row", "col"),
        check_vma=False,
    )
```

```python
import functools

import jax
import jax.numpy as jnp
from jax import lax
from jax.experimental import pallas as pl
from jax.experimental.pallas import tpu as pltpu
from jax.sharding import PartitionSpec as P

T = 128
N = 8 * T
F32 = jnp.float32
BF16 = jnp.bfloat16
STEP = 0.1
SECOND = 0.5 * STEP * STEP


def seven(kappa, flow_x, flow_y):
    edge = (4.0 / 6.0) * kappa
    corner = kappa / 6.0
    at = lax.broadcasted_iota(jnp.int32, kappa.shape, 1)

    def from_above(v):
        return jnp.where(at == 0, 0.0, pltpu.roll(v, 1, 1))

    def from_below(v):
        return jnp.where(at == T - 1, 0.0, pltpu.roll(v, T - 1, 1))

    return [
        (-20.0 / 6.0) * kappa,
        edge - 0.5 * flow_x,
        edge + 0.5 * flow_x,
        from_above(edge - 0.5 * flow_y),
        from_above(corner),
        from_below(edge + 0.5 * flow_y),
        from_below(corner),
    ]


def columns(lists):
    rows = list(lists)
    have = 8 * len(rows)
    if have < T:
        rows.append(jnp.zeros((T - have, T), F32))
    return jnp.concatenate(rows, axis=0).T


def spread(cols, j, x):
    return jnp.broadcast_to(cols[:, 8 * j + x : 8 * j + x + 1], (T, T))


def shifted(up, down, axis):
    return pltpu.roll(up, T - 1, axis) + pltpu.roll(down, 1, axis)


def full(mid, low, high, w, axis):
    both = low + high
    return w[0] * mid + w[1] * high + w[2] * low + shifted(w[3] * mid + w[4] * both, w[5] * mid + w[6] * both, axis)


def off(value, w, side, axis):
    return w[side] * value + shifted(w[4] * value, w[6] * value, axis)


def split(value):
    high = value.astype(BF16)
    return high, (value - high.astype(F32)).astype(BF16)


def times(value, weights):
    (vh, vl), (wh, wl) = split(value), weights
    dot = lambda a, b: jnp.dot(a, b, preferred_element_type=F32)
    return dot(vh, wh) + dot(vl, wh) + dot(vh, wl)


def right_factor(kuw, h, which):
    k, u, w = (v[h : h + 1, :] for v in kuw)
    i = lax.broadcasted_iota(jnp.int32, (T, T), 0)
    j = lax.broadcasted_iota(jnp.int32, (T, T), 1)
    edge = (4.0 / 6.0) * k
    if which == "own":
        mid, up, down = (-20.0 / 6.0) * k, edge - 0.5 * w, edge + 0.5 * w
    else:
        mid = edge - 0.5 * u if which == "next" else edge + 0.5 * u
        up = down = k / 6.0
    return jnp.where(i == j, mid, jnp.where(i == j + 1, up, jnp.where(i == j - 1, down, 0.0)))


def tables(ref):
    return ref[0:8, :], ref[8:16, :], ref[16:24, :]


def tile(i):
    return slice(i * T, (i + 1) * T)


def at_tile(i):
    return pl.ds(pl.multiple_of(i * T, T), T)


def call(body, out, scratch, ins, name, us):
    shapes = [jax.ShapeDtypeStruct(s, F32) for s, _ in out]
    specs = [space for _, space in out]
    return pl.pallas_call(
        body,
        in_specs=ins,
        out_specs=specs,
        out_shape=shapes,
        scratch_shapes=scratch,
        compiler_params=pltpu.CompilerParams(vmem_limit_bytes=40 << 20),
        cost_estimate=pl.CostEstimate(flops=us * 10**9, transcendentals=0, bytes_accessed=us * 3 * 10**6),
        name=name,
    )


VMEM = pl.BlockSpec(memory_space=pltpu.VMEM)
HBM = pl.BlockSpec(memory_space=pltpu.HBM)
DMA = pltpu.SemaphoreType.DMA
copy = pltpu.make_async_copy


def pack_body(p, k, u, w, left, right, kuw, sem):
    moves = [copy(v, kuw.at[pl.ds(8 * i, 8), :], sem.at[i]) for i, v in enumerate((k, u, w))]
    moves += [copy(p.at[:, pl.ds(7 * T * s, T)], out, sem.at[3 + s]) for s, out in enumerate((left, right))]
    for m in moves:
        m.start()
    for m in moves:
        m.wait()


def pack(cov, k, u, w):
    edge = ((N, T), VMEM)
    return call(pack_body, [edge, edge, ((24, T), VMEM)], [DMA((5,))], [HBM] * 4, "pack", 1)(cov, k, u, w)


def row_edges_body(p, q, kuw, top, bottom, wide, pb, sem):
    moves = []
    for i, out in enumerate((top, bottom)):
        moves.append(copy(p.at[pl.ds(7 * T * i, T), :], out.at[pl.ds(0, T), :], sem.at[3 * i]))
        moves.append(copy(q.at[pl.ds(7 * T * i, T), :], out.at[pl.ds(T, T), :], sem.at[3 * i + 1]))
        moves.append(copy(p.at[pl.ds(T + 5 * T * i, T), :], pb.at[i], sem.at[3 * i + 2]))
    for m in moves:
        m.start()
    cols = columns(seven(*tables(kuw)))
    for x in range(8):
        for j in range(7):
            wide[x, j] = spread(cols, j, x)
    for i, x, side, out in ((0, 0, 1, top), (1, 7, 2, bottom)):
        out[2 * T : 2 * T + 8, :] = jnp.zeros((8, N), F32)
        out[2 * T : 2 * T + 1, 0:T] = kuw[x : x + 1, :]
        out[2 * T : 2 * T + 1, T : 2 * T] = kuw[8 + x : 9 + x, :]
        for m in moves[3 * i : 3 * i + 3]:
            m.wait()

        @pl.loop(0, 8, unroll=8)
        def _(h):
            lanes = at_tile(h)
            m, n = out[0:T, lanes], pb[i, :, lanes]
            e = [wide[x, j] for j in range(7)]
            both = shifted(e[3] * m + e[4] * n, e[5] * m + e[6] * n, 0)
            out[T : 2 * T, lanes] = out[T : 2 * T, lanes] + (e[0] * m + e[side] * n + both)


def row_edges(cov, noise, kuw):
    edge = ((2 * T + 8, N), VMEM)
    scratch = [pltpu.VMEM((2, T, N), F32), DMA((6,))]
    return call(row_edges_body, [edge, edge, ((8, 7, T, T), VMEM)], scratch, [HBM, HBM, VMEM], "row_edges", 2)(cov, noise, kuw)


def row_finish_body(top, bottom, yl, yr, cw, top_out, bottom_out):
    v = seven(*tables(cw))
    for i, (src, out) in enumerate(((top, top_out), (bottom, bottom_out))):
        rows = pl.ds(7 * T * i, T)
        out[0:T, :] = src[0:T, :]
        out[2 * T : 2 * T + 8, :] = src[2 * T : 2 * T + 8, :]
        for h in range(8):
            low = 2.0 * yl[rows, :] if h == 0 else src[0:T, tile(h - 1)]
            high = 2.0 * yr[rows, :] if h == 7 else src[0:T, tile(h + 1)]
            term = full(src[0:T, tile(h)], low, high, [a[h : h + 1, :] for a in v], 1)
            out[T : 2 * T, tile(h)] = src[T : 2 * T, tile(h)] + term


def row_finish(top, bottom, yl, yr, cw):
    edge = ((2 * T + 8, N), VMEM)
    return call(row_finish_body, [edge, edge], [], [VMEM] * 5, "row_finish", 2)(top, bottom, yl, yr, cw)


def col_edges_body(p, q, wide, cw, left, right, pb, qb, sem):
    moves = []
    for s in range(2):
        moves.append(copy(p.at[:, pl.ds(6 * T * s, 2 * T)], pb.at[s], sem.at[2 * s]))
        moves.append(copy(q.at[:, pl.ds(7 * T * s, T)], qb.at[s], sem.at[2 * s + 1]))
    for m in moves:
        m.start()
    kuw = tables(cw)
    zero = jnp.zeros((T, T), F32)
    for s, h, out in ((0, 0, left), (1, 7, right)):
        out[N : N + 8, :] = jnp.zeros((8, T), F32)
        for i in range(2):
            out[N + i : N + i + 1, :] = kuw[i][h : h + 1, :]
        near, far = right_factor(kuw, h, "own"), right_factor(kuw, h, "before" if s else "next")
        factor = split(jnp.concatenate([far, near] if s else [near, far], axis=0))
        moves[2 * s].wait()
        moves[2 * s + 1].wait()
        mine = tile(s)
        out[0:N, :] = times(pb[s], factor)
        for x in range(8):
            e = [wide[x, j] for j in range(7)]
            low = zero if x == 0 else pb[s, tile(x - 1), mine]
            high = zero if x == 7 else pb[s, tile(x + 1), mine]
            out[tile(x), :] = out[tile(x), :] + (qb[s, tile(x), :] + full(pb[s, tile(x), mine], low, high, e, 0))


def col_edges(cov, noise, wide, cw):
    edge = ((N + 8, T), VMEM)
    scratch = [pltpu.VMEM((2, N, 2 * T), F32), pltpu.VMEM((2, N, T), F32), DMA((4,))]
    return call(col_edges_body, [edge, edge], scratch, [HBM, HBM] + [VMEM] * 2, "col_edges", 3)(cov, noise, wide, cw)


def block_body(p_hbm, q_hbm, yl, yr, wide, cw, o, pe, fe, v_s, sem_p, sem_q):
    def load_p(x):
        return copy(p_hbm.at[tile(x), :], pe.at[pl.ds((x + 1) * T, T), pl.ds(T, N)], sem_p.at[x])

    def load_q(x):
        return copy(q_hbm.at[tile(x), :], o.at[tile(x), :], sem_q.at[x])

    for x in range(8):
        load_p(x).start()
        load_q(x).start()
    inner = slice(T, 9 * T)
    pe[inner, 0:T] = yl[...]
    pe[inner, 9 * T : 10 * T] = yr[...]
    fe[inner, 0:T] = jnp.zeros((N, T), F32)
    fe[inner, 9 * T : 10 * T] = jnp.zeros((N, T), F32)
    for r in (pe, fe):
        r[0:T, inner] = jnp.zeros((T, N), F32)
        r[9 * T : 10 * T, inner] = jnp.zeros((T, N), F32)
    v = seven(*tables(cw))
    for x in range(8):
        for j in range(7):
            v_s[0, x, j] = jnp.broadcast_to(v[j][x : x + 1, :], (8, T))
        v_s[1, x, 0] = jnp.broadcast_to(v[0][x : x + 1, :] + STEP / SECOND, (8, T))
        for j in range(1, 7):
            v_s[1, x, j] = v_s[0, x, j]

    def apply(src, x, h, stage):
        e = [wide[x, j] for j in range(7)]
        v = [v_s[stage, h, j, 0:1, :] for j in range(7)]
        rows = pl.ds((x + 1) * T, T)
        mid, low, high = (src[rows, at_tile(h + i)] for i in (1, 0, 2))
        both = low + high
        value = (e[0] + v[0]) * mid + v[1] * high + v[2] * low
        value = value + shifted(v[3] * mid + v[4] * both, v[5] * mid + v[6] * both, 1)
        low, high = (src[pl.ds((x + i) * T, T), at_tile(h + 1)] for i in (0, 2))
        both = low + high
        value = value + e[1] * high + e[2] * low
        return value + shifted(e[3] * mid + e[4] * both, e[5] * mid + e[6] * both, 0)

    def first(x):
        @pl.loop(0, 8, unroll=8)
        def _(h):
            fe[pl.ds((x + 1) * T, T), at_tile(h + 1)] = o[tile(x), at_tile(h)] + apply(pe, x, h, 0)

    def second(x):
        @pl.loop(0, 8, unroll=8)
        def _(h):
            o[tile(x), at_tile(h)] = pe[pl.ds((x + 1) * T, T), at_tile(h + 1)] + SECOND * apply(fe, x, h, 1)

    load_p(0).wait()
    for x in range(9):
        if x < 8:
            if x < 7:
                load_p(x + 1).wait()
            load_q(x).wait()
            first(x)
        if x > 0:
            second(x - 1)


def block(cov, noise, yl, yr, wide, cw):
    scratch = [
        pltpu.VMEM((10 * T, 10 * T), F32),
        pltpu.VMEM((10 * T, 10 * T), F32),
        pltpu.VMEM((2, 8, 7, 8, T), F32),
        DMA((8,)),
        DMA((8,)),
    ]
    return call(block_body, [((N, N), VMEM)], scratch, [HBM, HBM] + [VMEM] * 4, "block", 16)(cov, noise, yl, yr, wide, cw)[0]


def halo_body(o, top, bottom, left, right, ru, rd, fl, fr, wide, cw, out, cb, rb, d, theirs, sem):
    inner = copy(o.at[pl.ds(2 * T, 4 * T), pl.ds(T, 6 * T)], out.at[pl.ds(2 * T, 4 * T), pl.ds(T, 6 * T)], sem.at[0])
    inner.start()
    saves = [inner]
    v = seven(*tables(cw))
    for s, (f, mine, h, toward, back) in enumerate(((fl, left, 0, 2, 1), (fr, right, 7, 1, 2))):
        spot = lambda i: jnp.broadcast_to(f[N + i : N + i + 1, :], (8, T))
        b = [a[0:1, :] for a in seven(spot(0), spot(1), jnp.zeros((8, T), F32))]
        vh = [a[h : h + 1, :] for a in v]
        for x in range(8):
            beside = f[tile(x), :] + off(mine[tile(x), :], b, back, 1)
            cb[s, tile(x), :] = o[tile(x), tile(h)] + SECOND * off(beside, vh, toward, 1)
        rows = pl.ds(2 * T, 4 * T)
        saves.append(copy(cb.at[s, rows, :], out.at[rows, pl.ds(7 * T * s, T)], sem.at[1 + s]))
        saves[-1].start()
    zero = jnp.zeros((T, T), F32)
    for i, (r, mine, x, x2, toward, back) in enumerate(((ru, top, 0, 1, 2, 1), (rd, bottom, 7, 6, 1, 2))):
        spot = lambda a: jnp.broadcast_to(r[2 * T : 2 * T + 1, a * T : (a + 1) * T], (8, T))
        cols = columns(seven(spot(0), spot(1), jnp.zeros((8, T), F32)))
        for j in (back, 4, 6):
            theirs[j] = spread(cols, j, 0)
        e = [wide[x, j] for j in range(7)]
        e2 = [wide[x2, j] for j in range(7)]
        b = [theirs[j] for j in range(7)]
        for h in range(8):
            d[:, tile(h)] = off(r[0:T, tile(h)], e, toward, 0)
        for h in range(8):
            vh = [a[h : h + 1, :] for a in v]
            mid = d[:, tile(h)]
            low = d[:, tile(h - 1)] if h > 0 else zero
            high = d[:, tile(h + 1)] if h < 7 else zero
            beside = r[T : 2 * T, tile(h)] + off(mine[0:T, tile(h)], b, back, 0)
            both = low + high
            value = (e[0] + (vh[0] + STEP / SECOND)) * mid + e[toward] * beside + vh[1] * high + vh[2] * low
            value = value + shifted(vh[3] * mid + vh[4] * both, vh[5] * mid + vh[6] * both, 1)
            value = value + shifted(e[3] * mid + e[4] * beside, e[5] * mid + e[6] * beside, 0)
            old = lambda at: cb[h // 7, tile(at), :] if h in (0, 7) else o[tile(at), tile(h)]
            rb[i, tile(i), tile(h)] = old(x) + SECOND * value
            rb[i, tile(1 - i), tile(h)] = old(x2) + SECOND * off(mid, e2, toward, 0)
        saves.append(copy(rb.at[i], out.at[pl.ds(6 * T * i, 2 * T), :], sem.at[3 + i]))
        saves[-1].start()
    for m in saves:
        m.wait()


def halo(o, top, bottom, left, right, ru, rd, fl, fr, wide, cw):
    scratch = [pltpu.VMEM((2, N, T), F32), pltpu.VMEM((2, 2 * T, N), F32), pltpu.VMEM((T, N), F32), pltpu.VMEM((7, T, T), F32), DMA((5,))]
    return call(halo_body, [((N, N), HBM)], scratch, [VMEM] * 11, "halo", 5)(o, top, bottom, left, right, ru, rd, fl, fr, wide, cw)[0]


@functools.cache
def weight_route(n):
    def place(r, c):
        half = n // 2
        return (2 * (c // half) + r // half, (c % half) // 2, r % half, c % 2)

    def far(a, b):
        ring = lambda d, size: min(d % size, -d % size)
        return ring(a[0] - b[0], 4) + ring(a[1] - b[1], max(n // 4, 1)) + ring(a[2] - b[2], n // 2) + 0.5 * (a[3] != b[3])

    pairs = []
    for c in range(n):
        cost = [[far(place(r, c), place(c, f)) for f in range(n)] for r in range(n)]
        for limit in sorted({x for row in cost for x in row}):
            taken = {}

            def find(r, seen):
                for f in sorted(range(n), key=lambda f: cost[r][f]):
                    if cost[r][f] <= limit and f not in seen:
                        seen.add(f)
                        if f not in taken or find(taken[f], seen):
                            taken[f] = r
                            return True
                return False

            if all(find(r, set()) for r in range(n)):
                break
        pairs += [(c * n + f, r * n + c) for f, r in taken.items()]
    return sorted(pairs)


def per_device(cov, noise, k, u, w):
    n_row, n_col = lax.axis_size("row"), lax.axis_size("col")

    def onward(a, axis, n):
        return lax.ppermute(a, axis, [(i, i + 1) for i in range(n - 1)])

    def back(a, axis, n):
        return lax.ppermute(a, axis, [(i + 1, i) for i in range(n - 1)])

    cov, noise, k, u, w = (pltpu.with_memory_space_constraint(a, pltpu.HBM) for a in (cov, noise, k, u, w))
    left, right, kuw = pack(cov, k, u, w)
    cw = lax.ppermute(kuw, ("row", "col"), weight_route(n_row))
    yl = onward(right, "col", n_col)
    yr = back(left, "col", n_col)
    top, bottom, wide = row_edges(cov, noise, kuw)
    top, bottom = row_finish(top, bottom, yl, yr, cw)
    ru = onward(bottom, "row", n_row)
    rd = back(top, "row", n_row)
    wide, top, bottom = lax.optimization_barrier((wide, top, bottom))
    left_f, right_f = col_edges(cov, noise, wide, cw)
    fl = onward(right_f, "col", n_col)
    fr = back(left_f, "col", n_col)
    o = block(cov, noise, yl, yr, wide, cw)
    return halo(o, top, bottom, left, right, ru, rd, fl, fr, wide, cw)


def solution(mesh):
    return jax.shard_map(
        per_device,
        mesh=mesh,
        in_specs=(P("row", "col"), P("row", "col"), P("row", None), P("row", None), P("row", None)),
        out_specs=P("row", "col"),
        check_vma=False,
    )
```

```python
import functools

import jax
import jax.numpy as jnp
from jax import lax
from jax.experimental import pallas as pl
from jax.experimental.pallas import tpu as pltpu
from jax.sharding import PartitionSpec as P

T = 128
N = 8 * T
F32 = jnp.float32
BF16 = jnp.bfloat16
STEP = 0.1
SECOND = 0.5 * STEP * STEP


def seven(kappa, flow_x, flow_y):
    edge = (4.0 / 6.0) * kappa
    corner = kappa / 6.0
    at = lax.broadcasted_iota(jnp.int32, kappa.shape, 1)

    def from_above(v):
        return jnp.where(at == 0, 0.0, pltpu.roll(v, 1, 1))

    def from_below(v):
        return jnp.where(at == T - 1, 0.0, pltpu.roll(v, T - 1, 1))

    return [
        (-20.0 / 6.0) * kappa,
        edge - 0.5 * flow_x,
        edge + 0.5 * flow_x,
        from_above(edge - 0.5 * flow_y),
        from_above(corner),
        from_below(edge + 0.5 * flow_y),
        from_below(corner),
    ]


def columns(lists):
    rows = list(lists)
    have = 8 * len(rows)
    if have < T:
        rows.append(jnp.zeros((T - have, T), F32))
    return jnp.concatenate(rows, axis=0).T


def spread(cols, j, x):
    return jnp.broadcast_to(cols[:, 8 * j + x : 8 * j + x + 1], (T, T))


def shifted(up, down, axis):
    return pltpu.roll(up, T - 1, axis) + pltpu.roll(down, 1, axis)


def full(mid, low, high, w, axis):
    both = low + high
    return w[0] * mid + w[1] * high + w[2] * low + shifted(w[3] * mid + w[4] * both, w[5] * mid + w[6] * both, axis)


def stencil(mid, above, below, left, right, e, v):
    value = (e[0] + v[0]) * mid
    for low, high, w, axis in ((left, right, v, 1), (above, below, e, 0)):
        both = low if high is None else high if low is None else low + high
        if high is not None:
            value = value + w[1] * high
        if low is not None:
            value = value + w[2] * low
        value = value + shifted(w[3] * mid + w[4] * both, w[5] * mid + w[6] * both, axis)
    return value


def off(value, w, side, axis):
    return w[side] * value + shifted(w[4] * value, w[6] * value, axis)


def split(value):
    high = value.astype(BF16)
    return high, (value - high.astype(F32)).astype(BF16)


def times(value, weights):
    (vh, vl), (wh, wl) = split(value), weights
    dot = lambda a, b: jnp.dot(a, b, preferred_element_type=F32)
    return dot(vh, wh) + dot(vl, wh) + dot(vh, wl)


def right_factor(kuw, h, which):
    k, u, w = (v[h : h + 1, :] for v in kuw)
    i = lax.broadcasted_iota(jnp.int32, (T, T), 0)
    j = lax.broadcasted_iota(jnp.int32, (T, T), 1)
    edge = (4.0 / 6.0) * k
    if which == "own":
        mid, up, down = (-20.0 / 6.0) * k, edge - 0.5 * w, edge + 0.5 * w
    else:
        mid = edge - 0.5 * u if which == "next" else edge + 0.5 * u
        up = down = k / 6.0
    return jnp.where(i == j, mid, jnp.where(i == j + 1, up, jnp.where(i == j - 1, down, 0.0)))


def tables(ref):
    return ref[0:8, :], ref[8:16, :], ref[16:24, :]


def tile(i):
    return slice(i * T, (i + 1) * T)


def at_tile(i):
    return pl.ds(pl.multiple_of(i * T, T), T)


def call(body, out, scratch, ins, name, us, aliases=None):
    shapes = [jax.ShapeDtypeStruct(s, F32) for s, _ in out]
    specs = [space for _, space in out]
    return pl.pallas_call(
        body,
        in_specs=ins,
        out_specs=specs,
        out_shape=shapes,
        scratch_shapes=scratch,
        input_output_aliases=aliases or {},
        compiler_params=pltpu.CompilerParams(vmem_limit_bytes=14 << 20),
        cost_estimate=pl.CostEstimate(flops=us * 10**9, transcendentals=0, bytes_accessed=us * 3 * 10**6),
        name=name,
    )


VMEM = pl.BlockSpec(memory_space=pltpu.VMEM)
HBM = pl.BlockSpec(memory_space=pltpu.HBM)
DMA = pltpu.SemaphoreType.DMA
copy = pltpu.make_async_copy


def pack_body(p, k, u, w, left, right, kuw, sem):
    moves = [copy(v, kuw.at[pl.ds(8 * i, 8), :], sem.at[i]) for i, v in enumerate((k, u, w))]
    moves += [copy(p.at[:, pl.ds(7 * T * s, T)], out, sem.at[3 + s]) for s, out in enumerate((left, right))]
    for m in moves:
        m.start()
    for m in moves:
        m.wait()


def pack(cov, k, u, w):
    edge = ((N, T), VMEM)
    return call(pack_body, [edge, edge, ((24, T), VMEM)], [DMA((5,))], [HBM] * 4, "pack", 1)(cov, k, u, w)


def row_edges_body(p, q, kuw, top, bottom, wide, pb, sem):
    moves = []
    for i, out in enumerate((top, bottom)):
        moves.append(copy(p.at[pl.ds(7 * T * i, T), :], out.at[pl.ds(0, T), :], sem.at[3 * i]))
        moves.append(copy(q.at[pl.ds(7 * T * i, T), :], out.at[pl.ds(T, T), :], sem.at[3 * i + 1]))
        moves.append(copy(p.at[pl.ds(T + 5 * T * i, T), :], pb.at[i], sem.at[3 * i + 2]))
    for m in moves:
        m.start()
    cols = columns(seven(*tables(kuw)))
    for x in range(8):
        for j in range(7):
            wide[x, j] = spread(cols, j, x)
    for i, x, side, out in ((0, 0, 1, top), (1, 7, 2, bottom)):
        out[2 * T : 2 * T + 8, :] = jnp.zeros((8, N), F32)
        out[2 * T : 2 * T + 1, 0:T] = kuw[x : x + 1, :]
        out[2 * T : 2 * T + 1, T : 2 * T] = kuw[8 + x : 9 + x, :]
        for m in moves[3 * i : 3 * i + 3]:
            m.wait()

        @pl.loop(0, 8, unroll=8)
        def _(h):
            lanes = at_tile(h)
            m, n = out[0:T, lanes], pb[i, :, lanes]
            e = [wide[x, j] for j in range(7)]
            both = shifted(e[3] * m + e[4] * n, e[5] * m + e[6] * n, 0)
            out[T : 2 * T, lanes] = out[T : 2 * T, lanes] + (e[0] * m + e[side] * n + both)


def row_edges(cov, noise, kuw):
    edge = ((2 * T + 8, N), VMEM)
    scratch = [pltpu.VMEM((2, T, N), F32), DMA((6,))]
    return call(row_edges_body, [edge, edge, ((8, 7, T, T), VMEM)], scratch, [HBM, HBM, VMEM], "row_edges", 2)(cov, noise, kuw)


def row_finish_body(top, bottom, yl, yr, cw, top_out, bottom_out):
    v = seven(*tables(cw))
    for i, (src, out) in enumerate(((top, top_out), (bottom, bottom_out))):
        rows = pl.ds(7 * T * i, T)
        for h in range(8):
            low = 2.0 * yl[rows, :] if h == 0 else src[0:T, tile(h - 1)]
            high = 2.0 * yr[rows, :] if h == 7 else src[0:T, tile(h + 1)]
            term = full(src[0:T, tile(h)], low, high, [a[h : h + 1, :] for a in v], 1)
            out[T : 2 * T, tile(h)] = src[T : 2 * T, tile(h)] + term


def row_finish(top, bottom, yl, yr, cw):
    edge = ((2 * T + 8, N), VMEM)
    return call(row_finish_body, [edge, edge], [], [VMEM] * 5, "row_finish", 1, {0: 0, 1: 1})(top, bottom, yl, yr, cw)


def col_edges_body(p, q, wide, cw, left, right):
    kuw = tables(cw)
    zero = jnp.zeros((T, T), F32)
    for s, h, out in ((0, 0, left), (1, 7, right)):
        out[N : N + 8, :] = jnp.zeros((8, T), F32)
        for i in range(2):
            out[N + i : N + i + 1, :] = kuw[i][h : h + 1, :]
        near, far = right_factor(kuw, h, "own"), right_factor(kuw, h, "before" if s else "next")
        factor = split(jnp.concatenate([far, near] if s else [near, far], axis=0))
        out[0:N, :] = times(p[:, 6 * T * s : 6 * T * s + 2 * T], factor)
        for x in range(8):
            e = [wide[x, j] for j in range(7)]
            low = zero if x == 0 else p[tile(x - 1), tile(h)]
            high = zero if x == 7 else p[tile(x + 1), tile(h)]
            out[tile(x), :] = out[tile(x), :] + (q[tile(x), tile(h)] + full(p[tile(x), tile(h)], low, high, e, 0))


def col_edges(cov, noise, wide, cw):
    edge = ((N + 8, T), VMEM)
    return call(col_edges_body, [edge, edge], [], [VMEM] * 4, "col_edges", 2)(cov, noise, wide, cw)


def block_body(p, q, yl, yr, wide, cw, o, f):
    v = seven(*tables(cw))
    vs = [[a[h : h + 1, :] for a in v] for h in range(8)]
    vs2 = [[w[0] + STEP / SECOND] + w[1:] for w in vs]

    def apply(src, left, right, x, h, w):
        row = lambda i: src[tile(i), tile(h)] if 0 <= i < 8 else None
        col = lambda i: src[tile(x), tile(i)] if 0 <= i < 8 else (left if i < 0 else right)
        e = [wide[x, j] for j in range(7)]
        return stencil(row(x), row(x - 1), row(x + 1), col(h - 1), col(h + 1), e, w[h])

    for x in range(9):
        if x < 8:
            for h in range(8):
                f[tile(x), tile(h)] = q[tile(x), tile(h)] + apply(p, yl[tile(x), :], yr[tile(x), :], x, h, vs)
        if x > 0:
            for h in range(8):
                o[tile(x - 1), tile(h)] = p[tile(x - 1), tile(h)] + SECOND * apply(f, None, None, x - 1, h, vs2)


def block(cov, noise, yl, yr, wide, cw):
    return call(block_body, [((N, N), VMEM)], [pltpu.VMEM((N, N), F32)], [VMEM] * 6, "block", 12)(cov, noise, yl, yr, wide, cw)[0]


def row_halo_body(o_in, top, bottom, ru, rd, wide, cw, o, d, theirs):
    v = seven(*tables(cw))
    get = lambda ref, h: ref[0:T, tile(h)] if 0 <= h < 8 else jnp.zeros((T, T), F32)
    for r, mine, x, x2, toward, back in ((ru, top, 0, 1, 2, 1), (rd, bottom, 7, 6, 1, 2)):
        spot = lambda a: jnp.broadcast_to(r[2 * T : 2 * T + 1, a * T : (a + 1) * T], (8, T))
        cols = columns(seven(spot(0), spot(1), jnp.zeros((8, T), F32)))
        for j in (back, 4, 6):
            theirs[j] = spread(cols, j, 0)
        e = [wide[x, j] for j in range(7)]
        e2 = [wide[x2, j] for j in range(7)]
        b = [theirs[j] for j in range(7)]
        for h in range(8):
            d[:, tile(h)] = off(r[0:T, tile(h)], e, toward, 0)
        for h in range(8):
            vh = [a[h : h + 1, :] for a in v]
            mid = d[:, tile(h)]
            beside = r[T : 2 * T, tile(h)] + off(mine[0:T, tile(h)], b, back, 0)
            low, high = get(d, h - 1), get(d, h + 1)
            both = low + high
            value = (e[0] + (vh[0] + STEP / SECOND)) * mid + e[toward] * beside + vh[1] * high + vh[2] * low
            value = value + shifted(vh[3] * mid + vh[4] * both, vh[5] * mid + vh[6] * both, 1)
            value = value + shifted(e[3] * mid + e[4] * beside, e[5] * mid + e[6] * beside, 0)
            o[tile(x), tile(h)] = o_in[tile(x), tile(h)] + SECOND * value
            o[tile(x2), tile(h)] = o_in[tile(x2), tile(h)] + SECOND * off(mid, e2, toward, 0)


def row_halo(*args):
    scratch = [pltpu.VMEM((T, N), F32), pltpu.VMEM((7, T, T), F32)]
    return call(row_halo_body, [((N, N), VMEM)], scratch, [VMEM] * 7, "row_halo", 4, {0: 0})(*args)[0]


def col_halo_body(o, left, right, fl, fr, cw, out, cb, sem):
    inner = copy(o.at[:, pl.ds(T, 6 * T)], out.at[:, pl.ds(T, 6 * T)], sem.at[0])
    inner.start()
    saves = [inner]
    v = seven(*tables(cw))
    for s, (f, mine, h, toward, back) in enumerate(((fl, left, 0, 2, 1), (fr, right, 7, 1, 2))):
        spot = lambda i: jnp.broadcast_to(f[N + i : N + i + 1, :], (8, T))
        b = [a[0:1, :] for a in seven(spot(0), spot(1), jnp.zeros((8, T), F32))]
        vh = [a[h : h + 1, :] for a in v]
        for x in range(8):
            beside = f[tile(x), :] + off(mine[tile(x), :], b, back, 1)
            cb[s, tile(x), :] = o[tile(x), tile(h)] + SECOND * off(beside, vh, toward, 1)
        saves.append(copy(cb.at[s], out.at[:, pl.ds(7 * T * s, T)], sem.at[1 + s]))
        saves[-1].start()
    for m in saves:
        m.wait()


def col_halo(*args):
    scratch = [pltpu.VMEM((2, N, T), F32), DMA((3,))]
    return call(col_halo_body, [((N, N), HBM)], scratch, [VMEM] * 6, "col_halo", 2)(*args)[0]


@functools.cache
def weight_route(n):
    def place(r, c):
        half = n // 2
        return (2 * (c // half) + r // half, (c % half) // 2, r % half, c % 2)

    def far(a, b):
        ring = lambda d, size: min(d % size, -d % size)
        return ring(a[0] - b[0], 4) + ring(a[1] - b[1], max(n // 4, 1)) + ring(a[2] - b[2], n // 2) + 0.5 * (a[3] != b[3])

    pairs = []
    for c in range(n):
        cost = [[far(place(r, c), place(c, f)) for f in range(n)] for r in range(n)]
        for limit in sorted({x for row in cost for x in row}):
            taken = {}

            def find(r, seen):
                for f in sorted(range(n), key=lambda f: cost[r][f]):
                    if cost[r][f] <= limit and f not in seen:
                        seen.add(f)
                        if f not in taken or find(taken[f], seen):
                            taken[f] = r
                            return True
                return False

            if all(find(r, set()) for r in range(n)):
                break
        pairs += [(c * n + f, r * n + c) for f, r in taken.items()]
    return sorted(pairs)


def per_device(cov, noise, k, u, w):
    n_row, n_col = lax.axis_size("row"), lax.axis_size("col")

    def onward(a, axis, n):
        return lax.ppermute(a, axis, [(i, i + 1) for i in range(n - 1)])

    def back(a, axis, n):
        return lax.ppermute(a, axis, [(i + 1, i) for i in range(n - 1)])

    in_hbm = lambda a: pltpu.with_memory_space_constraint(a, pltpu.HBM)
    cov_hbm, noise_hbm = in_hbm(cov), in_hbm(noise)
    left, right, kuw = pack(cov_hbm, in_hbm(k), in_hbm(u), in_hbm(w))
    cw = lax.ppermute(kuw, ("row", "col"), weight_route(n_row))
    yl = onward(right, "col", n_col)
    yr = back(left, "col", n_col)
    top, bottom, wide = row_edges(cov_hbm, noise_hbm, kuw)
    top, bottom = row_finish(top, bottom, yl, yr, cw)
    ru = onward(bottom, "row", n_row)
    rd = back(top, "row", n_row)
    wide, top, bottom = lax.optimization_barrier((wide, top, bottom))
    left_f, right_f = col_edges(cov, noise, wide, cw)
    fl = onward(right_f, "col", n_col)
    fr = back(left_f, "col", n_col)
    o = block(cov, noise, yl, yr, wide, cw)
    o = row_halo(o, top, bottom, ru, rd, wide, cw)
    return col_halo(o, left, right, fl, fr, cw)


def solution(mesh):
    return jax.shard_map(
        per_device,
        mesh=mesh,
        in_specs=(P("row", "col"), P("row", "col"), P("row", None), P("row", None), P("row", None)),
        out_specs=P("row", "col"),
        check_vma=False,
    )
```

```python
import functools

import jax
import jax.numpy as jnp
from jax import lax
from jax.experimental import pallas as pl
from jax.experimental.pallas import tpu as pltpu
from jax.sharding import PartitionSpec as P

T = 128
N = 8 * T
F32 = jnp.float32
BF16 = jnp.bfloat16
STEP = 0.1
SECOND = 0.5 * STEP * STEP


def seven(kappa, flow_x, flow_y):
    edge = (4.0 / 6.0) * kappa
    corner = kappa / 6.0
    at = lax.broadcasted_iota(jnp.int32, kappa.shape, 1)

    def from_above(v):
        return jnp.where(at == 0, 0.0, pltpu.roll(v, 1, 1))

    def from_below(v):
        return jnp.where(at == T - 1, 0.0, pltpu.roll(v, T - 1, 1))

    return [
        (-20.0 / 6.0) * kappa,
        edge - 0.5 * flow_x,
        edge + 0.5 * flow_x,
        from_above(edge - 0.5 * flow_y),
        from_above(corner),
        from_below(edge + 0.5 * flow_y),
        from_below(corner),
    ]


def columns(lists):
    rows = list(lists)
    have = 8 * len(rows)
    if have < T:
        rows.append(jnp.zeros((T - have, T), F32))
    return jnp.concatenate(rows, axis=0).T


def spread(cols, j, x):
    return jnp.broadcast_to(cols[:, 8 * j + x : 8 * j + x + 1], (T, T))


def shifted(up, down, axis):
    return pltpu.roll(up, T - 1, axis) + pltpu.roll(down, 1, axis)


def full(mid, low, high, w, axis):
    both = low + high
    return w[0] * mid + w[1] * high + w[2] * low + shifted(w[3] * mid + w[4] * both, w[5] * mid + w[6] * both, axis)


def stencil(mid, above, below, left, right, e, v):
    value = (e[0] + v[0]) * mid
    for low, high, w, axis in ((left, right, v, 1), (above, below, e, 0)):
        both = low if high is None else high if low is None else low + high
        if high is not None:
            value = value + w[1] * high
        if low is not None:
            value = value + w[2] * low
        value = value + shifted(w[3] * mid + w[4] * both, w[5] * mid + w[6] * both, axis)
    return value


def off(value, w, side, axis):
    return w[side] * value + shifted(w[4] * value, w[6] * value, axis)


def split(value):
    high = value.astype(BF16)
    return high, (value - high.astype(F32)).astype(BF16)


def times(value, weights):
    (vh, vl), (wh, wl) = split(value), weights
    dot = lambda a, b: jnp.dot(a, b, preferred_element_type=F32)
    return dot(vh, wh) + dot(vl, wh) + dot(vh, wl)


def right_factor(kuw, h, which):
    k, u, w = (v[h : h + 1, :] for v in kuw)
    i = lax.broadcasted_iota(jnp.int32, (T, T), 0)
    j = lax.broadcasted_iota(jnp.int32, (T, T), 1)
    edge = (4.0 / 6.0) * k
    if which == "own":
        mid, up, down = (-20.0 / 6.0) * k, edge - 0.5 * w, edge + 0.5 * w
    else:
        mid = edge - 0.5 * u if which == "next" else edge + 0.5 * u
        up = down = k / 6.0
    return jnp.where(i == j, mid, jnp.where(i == j + 1, up, jnp.where(i == j - 1, down, 0.0)))


def tables(ref):
    return ref[0:8, :], ref[8:16, :], ref[16:24, :]


def tile(i):
    return slice(i * T, (i + 1) * T)


def at_tile(i):
    return pl.ds(pl.multiple_of(i * T, T), T)


def call(body, out, scratch, ins, name, us, aliases=None):
    shapes = [jax.ShapeDtypeStruct(s, F32) for s, _ in out]
    specs = [space for _, space in out]
    return pl.pallas_call(
        body,
        in_specs=ins,
        out_specs=specs,
        out_shape=shapes,
        scratch_shapes=scratch,
        input_output_aliases=aliases or {},
        compiler_params=pltpu.CompilerParams(vmem_limit_bytes=14 << 20),
        cost_estimate=pl.CostEstimate(flops=us * 10**9, transcendentals=0, bytes_accessed=us * 3 * 10**6),
        name=name,
    )


VMEM = pl.BlockSpec(memory_space=pltpu.VMEM)
HBM = pl.BlockSpec(memory_space=pltpu.HBM)
DMA = pltpu.SemaphoreType.DMA
copy = pltpu.make_async_copy


def pack_body(p, k, u, w, left, right, kuw, sem):
    moves = [copy(v, kuw.at[pl.ds(8 * i, 8), :], sem.at[i]) for i, v in enumerate((k, u, w))]
    moves += [copy(p.at[:, pl.ds(7 * T * s, T)], out, sem.at[3 + s]) for s, out in enumerate((left, right))]
    for m in moves:
        m.start()
    for m in moves:
        m.wait()


def pack(cov, k, u, w):
    edge = ((N, T), VMEM)
    return call(pack_body, [edge, edge, ((24, T), VMEM)], [DMA((5,))], [HBM] * 4, "pack", 1)(cov, k, u, w)


def row_edges_body(p, q, kuw, top, bottom, wide, pb, sem):
    moves = []
    for i, out in enumerate((top, bottom)):
        moves.append(copy(p.at[pl.ds(7 * T * i, T), :], out.at[pl.ds(0, T), :], sem.at[3 * i]))
        moves.append(copy(q.at[pl.ds(7 * T * i, T), :], out.at[pl.ds(T, T), :], sem.at[3 * i + 1]))
        moves.append(copy(p.at[pl.ds(T + 5 * T * i, T), :], pb.at[i], sem.at[3 * i + 2]))
    for m in moves:
        m.start()
    cols = columns(seven(*tables(kuw)))
    for x in range(8):
        for j in range(7):
            wide[x, j] = spread(cols, j, x)
    for i, x, side, out in ((0, 0, 1, top), (1, 7, 2, bottom)):
        out[2 * T : 2 * T + 8, :] = jnp.zeros((8, N), F32)
        out[2 * T : 2 * T + 1, 0:T] = kuw[x : x + 1, :]
        out[2 * T : 2 * T + 1, T : 2 * T] = kuw[8 + x : 9 + x, :]
        for m in moves[3 * i : 3 * i + 3]:
            m.wait()

        @pl.loop(0, 8, unroll=8)
        def _(h):
            lanes = at_tile(h)
            m, n = out[0:T, lanes], pb[i, :, lanes]
            e = [wide[x, j] for j in range(7)]
            both = shifted(e[3] * m + e[4] * n, e[5] * m + e[6] * n, 0)
            out[T : 2 * T, lanes] = out[T : 2 * T, lanes] + (e[0] * m + e[side] * n + both)


def row_edges(cov, noise, kuw):
    edge = ((2 * T + 8, N), VMEM)
    scratch = [pltpu.VMEM((2, T, N), F32), DMA((6,))]
    return call(row_edges_body, [edge, edge, ((8, 7, T, T), VMEM)], scratch, [HBM, HBM, VMEM], "row_edges", 2)(cov, noise, kuw)


def row_finish_body(top, bottom, yl, yr, cw, top_out, bottom_out):
    v = seven(*tables(cw))
    for i, (src, out) in enumerate(((top, top_out), (bottom, bottom_out))):
        rows = pl.ds(7 * T * i, T)
        out[0:T, :] = src[0:T, :]
        out[2 * T : 2 * T + 8, :] = src[2 * T : 2 * T + 8, :]
        for h in range(8):
            low = 2.0 * yl[rows, :] if h == 0 else src[0:T, tile(h - 1)]
            high = 2.0 * yr[rows, :] if h == 7 else src[0:T, tile(h + 1)]
            term = full(src[0:T, tile(h)], low, high, [a[h : h + 1, :] for a in v], 1)
            out[T : 2 * T, tile(h)] = src[T : 2 * T, tile(h)] + term


def row_finish(top, bottom, yl, yr, cw):
    edge = ((2 * T + 8, N), VMEM)
    return call(row_finish_body, [edge, edge], [], [VMEM] * 5, "row_finish", 1)(top, bottom, yl, yr, cw)


def col_edges_body(p, q, wide, cw, left, right):
    kuw = tables(cw)
    zero = jnp.zeros((T, T), F32)
    for s, h, out in ((0, 0, left), (1, 7, right)):
        out[N : N + 8, :] = jnp.zeros((8, T), F32)
        for i in range(2):
            out[N + i : N + i + 1, :] = kuw[i][h : h + 1, :]
        near, far = right_factor(kuw, h, "own"), right_factor(kuw, h, "before" if s else "next")
        factor = split(jnp.concatenate([far, near] if s else [near, far], axis=0))
        out[0:N, :] = times(p[:, 6 * T * s : 6 * T * s + 2 * T], factor)
        for x in range(8):
            e = [wide[x, j] for j in range(7)]
            low = zero if x == 0 else p[tile(x - 1), tile(h)]
            high = zero if x == 7 else p[tile(x + 1), tile(h)]
            out[tile(x), :] = out[tile(x), :] + (q[tile(x), tile(h)] + full(p[tile(x), tile(h)], low, high, e, 0))


def col_edges(cov, noise, wide, cw):
    edge = ((N + 8, T), VMEM)
    return call(col_edges_body, [edge, edge], [], [VMEM] * 4, "col_edges", 2)(cov, noise, wide, cw)


def block_body(p, q, yl, yr, wide, cw, o, f):
    v = seven(*tables(cw))
    vs = [[a[h : h + 1, :] for a in v] for h in range(8)]
    vs2 = [[w[0] + STEP / SECOND] + w[1:] for w in vs]

    def apply(src, left, right, x, h, w):
        row = lambda i: src[tile(i), tile(h)] if 0 <= i < 8 else None
        col = lambda i: src[tile(x), tile(i)] if 0 <= i < 8 else (left if i < 0 else right)
        e = [wide[x, j] for j in range(7)]
        return stencil(row(x), row(x - 1), row(x + 1), col(h - 1), col(h + 1), e, w[h])

    for x in range(9):
        if x < 8:
            for h in range(8):
                f[tile(x), tile(h)] = q[tile(x), tile(h)] + apply(p, yl[tile(x), :], yr[tile(x), :], x, h, vs)
        if x > 0:
            for h in range(8):
                o[tile(x - 1), tile(h)] = p[tile(x - 1), tile(h)] + SECOND * apply(f, None, None, x - 1, h, vs2)


def block(cov, noise, yl, yr, wide, cw):
    return call(block_body, [((N, N), VMEM)], [pltpu.VMEM((N, N), F32)], [VMEM] * 6, "block", 12)(cov, noise, yl, yr, wide, cw)[0]


def row_halo_body(o_in, top, bottom, ru, rd, wide, cw, o, d, theirs):
    v = seven(*tables(cw))
    get = lambda ref, h: ref[0:T, tile(h)] if 0 <= h < 8 else jnp.zeros((T, T), F32)
    for r, mine, x, x2, toward, back in ((ru, top, 0, 1, 2, 1), (rd, bottom, 7, 6, 1, 2)):
        spot = lambda a: jnp.broadcast_to(r[2 * T : 2 * T + 1, a * T : (a + 1) * T], (8, T))
        cols = columns(seven(spot(0), spot(1), jnp.zeros((8, T), F32)))
        for j in (back, 4, 6):
            theirs[j] = spread(cols, j, 0)
        e = [wide[x, j] for j in range(7)]
        e2 = [wide[x2, j] for j in range(7)]
        b = [theirs[j] for j in range(7)]
        for h in range(8):
            d[:, tile(h)] = off(r[0:T, tile(h)], e, toward, 0)
        for h in range(8):
            vh = [a[h : h + 1, :] for a in v]
            mid = d[:, tile(h)]
            beside = r[T : 2 * T, tile(h)] + off(mine[0:T, tile(h)], b, back, 0)
            low, high = get(d, h - 1), get(d, h + 1)
            both = low + high
            value = (e[0] + (vh[0] + STEP / SECOND)) * mid + e[toward] * beside + vh[1] * high + vh[2] * low
            value = value + shifted(vh[3] * mid + vh[4] * both, vh[5] * mid + vh[6] * both, 1)
            value = value + shifted(e[3] * mid + e[4] * beside, e[5] * mid + e[6] * beside, 0)
            o[tile(x), tile(h)] = o_in[tile(x), tile(h)] + SECOND * value
            o[tile(x2), tile(h)] = o_in[tile(x2), tile(h)] + SECOND * off(mid, e2, toward, 0)


def row_halo(*args):
    scratch = [pltpu.VMEM((T, N), F32), pltpu.VMEM((7, T, T), F32)]
    return call(row_halo_body, [((N, N), VMEM)], scratch, [VMEM] * 7, "row_halo", 4, {0: 0})(*args)[0]


def col_halo_body(o, left, right, fl, fr, cw, out, cb, sem):
    inner = copy(o.at[:, pl.ds(T, 6 * T)], out.at[:, pl.ds(T, 6 * T)], sem.at[0])
    inner.start()
    saves = [inner]
    v = seven(*tables(cw))
    for s, (f, mine, h, toward, back) in enumerate(((fl, left, 0, 2, 1), (fr, right, 7, 1, 2))):
        spot = lambda i: jnp.broadcast_to(f[N + i : N + i + 1, :], (8, T))
        b = [a[0:1, :] for a in seven(spot(0), spot(1), jnp.zeros((8, T), F32))]
        vh = [a[h : h + 1, :] for a in v]
        for x in range(8):
            beside = f[tile(x), :] + off(mine[tile(x), :], b, back, 1)
            cb[s, tile(x), :] = o[tile(x), tile(h)] + SECOND * off(beside, vh, toward, 1)
            if x % 4 == 3:
                rows = pl.ds((x - 3) * T, 4 * T)
                saves.append(copy(cb.at[s, rows, :], out.at[rows, pl.ds(7 * T * s, T)], sem.at[len(saves)]))
                saves[-1].start()
    for m in saves:
        m.wait()


def col_halo(*args):
    scratch = [pltpu.VMEM((2, N, T), F32), DMA((5,))]
    return call(col_halo_body, [((N, N), HBM)], scratch, [VMEM] * 6, "col_halo", 2)(*args)[0]


@functools.cache
def weight_route(n):
    def place(r, c):
        half = n // 2
        return (2 * (c // half) + r // half, (c % half) // 2, r % half, c % 2)

    def far(a, b):
        ring = lambda d, size: min(d % size, -d % size)
        return ring(a[0] - b[0], 4) + ring(a[1] - b[1], max(n // 4, 1)) + ring(a[2] - b[2], n // 2) + 0.5 * (a[3] != b[3])

    pairs = []
    for c in range(n):
        cost = [[far(place(r, c), place(c, f)) for f in range(n)] for r in range(n)]
        for limit in sorted({x for row in cost for x in row}):
            taken = {}

            def find(r, seen):
                for f in sorted(range(n), key=lambda f: cost[r][f]):
                    if cost[r][f] <= limit and f not in seen:
                        seen.add(f)
                        if f not in taken or find(taken[f], seen):
                            taken[f] = r
                            return True
                return False

            if all(find(r, set()) for r in range(n)):
                break
        pairs += [(c * n + f, r * n + c) for f, r in taken.items()]
    return sorted(pairs)


def per_device(cov, noise, k, u, w):
    n_row, n_col = lax.axis_size("row"), lax.axis_size("col")

    def onward(a, axis, n):
        return lax.ppermute(a, axis, [(i, i + 1) for i in range(n - 1)])

    def back(a, axis, n):
        return lax.ppermute(a, axis, [(i + 1, i) for i in range(n - 1)])

    in_hbm = lambda a: pltpu.with_memory_space_constraint(a, pltpu.HBM)
    cov_hbm, noise_hbm = in_hbm(cov), in_hbm(noise)
    left, right, kuw = pack(cov_hbm, in_hbm(k), in_hbm(u), in_hbm(w))
    cw = lax.ppermute(kuw, ("row", "col"), weight_route(n_row))
    yl = onward(right, "col", n_col)
    yr = back(left, "col", n_col)
    top, bottom, wide = row_edges(cov_hbm, noise_hbm, kuw)
    top, bottom = row_finish(top, bottom, yl, yr, cw)
    ru = onward(bottom, "row", n_row)
    rd = back(top, "row", n_row)
    wide, top, bottom = lax.optimization_barrier((wide, top, bottom))
    left_f, right_f = col_edges(cov, noise, wide, cw)
    fl = onward(right_f, "col", n_col)
    fr = back(left_f, "col", n_col)
    o = block(cov, noise, yl, yr, wide, cw)
    o = row_halo(o, top, bottom, ru, rd, wide, cw)
    return col_halo(o, left, right, fl, fr, cw)


def solution(mesh):
    return jax.shard_map(
        per_device,
        mesh=mesh,
        in_specs=(P("row", "col"), P("row", "col"), P("row", None), P("row", None), P("row", None)),
        out_specs=P("row", "col"),
        check_vma=False,
    )
```
